32 devices in a mesh: line: 2 (over x), track: 16 (over z, y, core).
Axes of the slice: x: 2, y: 2, z: 4, core: 2. Of those that a mesh axis runs over, the one named last changes fastest.
Arguments:
- radiance: bfloat16 [2, 64, 224, 1000], P('line', 'track'), may hold values from -40 to 40, as said below
Outputs:
- cleaned: bfloat16 [2, 64, 224, 1000], P('line', 'track')
- filter_matrix: float32 [224, 224], replicated
The draws below stay inside these ranges and needn't reach their ends.
Inputs may be any that keep to these rules, and one draw needn't show every extreme that they name: `radiance`: every flightline, band and column carries a column offset, a column gain and pixel noise, so no column is constant along track.
All inputs are finite; a program needn't handle non-finite values.
Results may differ from the reference program's by a relative error of at most 0.0045.
Values may be sent and summed in bfloat16 or wider, within the bound.
A program may use at most 64 MiB of HBM per device.

```python
import math
import jax
import jax.numpy as jnp
from jax import lax

BANDS = 224
COLS = 1000
NCOMP = 40
ITERS = 4
ROWS = 64
LINES = 2


def draw_radiance(key, part):
    line_axis = jnp.arange(LINES, dtype=jnp.float32)[:, None, None, None]
    row_axis = jnp.arange(ROWS, dtype=jnp.float32)[None, :, None, None]
    band_axis = jnp.arange(BANDS, dtype=jnp.float32)[None, None, :, None]
    scene = jnp.zeros((LINES, ROWS, BANDS, COLS), jnp.float32)
    for term in range(8):
        sub_keys = jax.random.split(jax.random.fold_in(key, term + 1), 5)
        amplitude = jax.random.normal(sub_keys[0], (LINES, 1, 1, COLS), jnp.float32)
        column_phase = jax.random.uniform(sub_keys[1], (LINES, 1, 1, COLS), jnp.float32, 0.0, 6.2831853)
        along_rate = jax.random.uniform(sub_keys[2], (LINES, 1, 1, 1), jnp.float32, 0.02, 0.1)
        band_rate = jax.random.uniform(sub_keys[3], (LINES, 1, 1, 1), jnp.float32, 0.5, 1.5) * (term + 1)
        band_phase = jax.random.uniform(sub_keys[4], (LINES, 1, 1, 1), jnp.float32, 0.0, 6.2831853)
        scene = scene + amplitude * jnp.cos(along_rate * row_axis + column_phase) * jnp.cos(3.14159265 * band_rate * band_axis / BANDS + band_phase)
    base_keys = jax.random.split(jax.random.fold_in(key, 100), 4)
    noise_level = jnp.exp(jax.random.uniform(base_keys[0], (LINES, 1, BANDS, 1), jnp.float32, math.log(0.15), math.log(0.6)))
    jitter = jax.random.normal(base_keys[1], (LINES, ROWS, BANDS, COLS), jnp.float32)
    ramp = (1.0 + 2.0 * row_axis / (ROWS - 1)) * (1.0 + 2.0 * line_axis / (LINES - 1))
    offset = 2.0 * jax.random.normal(base_keys[2], (LINES, 1, BANDS, COLS), jnp.float32)
    gain_map = jnp.exp(jax.random.uniform(base_keys[3], (LINES, 1, BANDS, COLS), jnp.float32, -0.5, 0.5))
    values = offset + gain_map * 0.4 * ramp * (0.5 * scene + noise_level * jitter)
    return jnp.clip(values, -40.0, 40.0).astype(jnp.bfloat16)


def setup_inputs(seed: int = 0) -> dict:
    seeds = jax.random.split(jax.random.key(seed), 2)
    return {
        "radiance": draw_radiance(jax.random.fold_in(seeds[1], 71), 0),
    }


EPSILON = 1e-05
HIGHEST = lax.Precision.HIGHEST

def destripe(flight_line):
    values = flight_line.astype(jnp.float32)
    first_sum = lax.optimization_barrier(jnp.sum(values, axis=0))
    second_sum = lax.optimization_barrier(jnp.sum(values * values, axis=0))
    col_mean = first_sum / ROWS
    col_spread = jnp.sqrt(second_sum / ROWS - col_mean * col_mean + EPSILON)
    band_mean = lax.optimization_barrier(jnp.mean(col_mean, axis=1))
    factor = lax.optimization_barrier(jnp.mean(col_spread, axis=1))[:, None] / col_spread
    centred = lax.optimization_barrier(((values - col_mean) * factor).astype(jnp.bfloat16))
    return (centred, band_mean)

def line_grams(flight_line):
    centred, band_mean = destripe(flight_line)
    widened = centred.astype(jnp.float32)
    steps_along = lax.optimization_barrier((widened[1:] - widened[:-1]).astype(jnp.bfloat16)).astype(jnp.float32)
    signal_part = jnp.einsum('rbc,rdc->bd', widened, widened)
    noise_part = jnp.einsum('rbc,rdc->bd', steps_along, steps_along)
    return (signal_part, noise_part)

def mnf_filter(signal_gram, noise_gram):
    noise_factor = jnp.linalg.cholesky(noise_gram)
    half_solved = jax.scipy.linalg.solve_triangular(noise_factor, signal_gram, lower=True)
    whitened = jax.scipy.linalg.solve_triangular(noise_factor, half_solved.T, lower=True)
    whitened = 0.5 * (whitened + whitened.T)
    subspace = jnp.eye(whitened.shape[0], NCOMP, dtype=jnp.float32)
    for iteration in range(ITERS):
        mapped = jnp.dot(whitened, subspace, precision=HIGHEST)
        inner_gram = jnp.dot(mapped.T, mapped, precision=HIGHEST)
        inner_factor = jnp.linalg.cholesky(inner_gram)
        subspace = jax.scipy.linalg.solve_triangular(inner_factor, mapped.T, lower=True).T
    forward_map = jax.scipy.linalg.solve_triangular(noise_factor.T, subspace, lower=False)
    backward_map = jnp.dot(noise_factor, subspace, precision=HIGHEST)
    return jnp.dot(forward_map, backward_map.T, precision=HIGHEST)

def reference(radiance):
    signal_parts, noise_parts = lax.map(line_grams, radiance)
    signal_gram = lax.optimization_barrier(jnp.sum(signal_parts, axis=0)) / (LINES * ROWS * COLS)
    noise_gram = lax.optimization_barrier(jnp.sum(noise_parts, axis=0)) / (2 * LINES * (ROWS - 1) * COLS)
    filter_matrix = mnf_filter(signal_gram, noise_gram)
    narrow = lax.optimization_barrier(filter_matrix.astype(jnp.bfloat16)).astype(jnp.float32)

    def restore(flight_line):
        centred, band_mean = destripe(flight_line)
        mixed = jnp.einsum('ab,rac->rbc', narrow, centred.astype(jnp.float32))
        return (band_mean[:, None] + mixed).astype(jnp.bfloat16)
    cleaned = lax.map(restore, radiance)
    return (cleaned, filter_matrix)
```

```python
import functools

import jax
import jax.numpy as jnp
from jax import lax
from jax.experimental import pallas as pl
from jax.experimental.pallas import tpu as pltpu
from jax.sharding import PartitionSpec as P

NCOMP = 40
ITERS = 4


EPSILON = 1e-05
HIGHEST = lax.Precision.HIGHEST


def from_behind(block, axis, distance):
    devices = range(lax.axis_size(axis))
    route = [(i - distance, i) for i in devices if i - distance in devices]
    return lax.ppermute(block, axis, route)


def column_terms(first_total, second_total, total_rows):
    col_mean = first_total / total_rows
    col_spread = jnp.sqrt(second_total / total_rows - col_mean * col_mean + EPSILON)
    band_mean = jnp.mean(col_mean, axis=1)
    factor = jnp.mean(col_spread, axis=1)[:, None] / col_spread
    return (col_mean, factor, band_mean)


PANEL = 32
GROUP = 8


def contract(left, right, left_axis, right_axis):
    return lax.dot_general(
        left, right, (((left_axis,), (right_axis,)), ((), ())),
        precision=HIGHEST, preferred_element_type=jnp.float32,
    )


def eliminate(panel, offset):
    size = panel.shape[0]
    row_ids = lax.broadcasted_iota(jnp.int32, (size, 128), 0)
    repeats = panel.shape[1] // 128
    tiles = [panel[:, t * 128:(t + 1) * 128] for t in range(repeats)]
    home, shift = divmod(offset, 128)
    scales = jnp.zeros((size, 128), jnp.float32)
    for start in range(0, size, GROUP):
        lanes = range(start, min(start + GROUP, size))
        columns = {}
        for k in lanes:
            tile, lane = divmod(offset + k, 128)
            columns[k] = jnp.broadcast_to(tiles[tile][:, lane:lane + 1], (size, 128))
        for k in lanes:
            pivot_row = jnp.broadcast_to(columns[k][k:k + 1], (size, 128))
            scales = jnp.where(row_ids == k, pivot_row, scales)
            step = jnp.where(row_ids > k, columns[k] * (1.0 / pivot_row), 0.0)
            for later in lanes:
                if later > k:
                    columns[later] = columns[later] - step * columns[later][k:k + 1]
            tiles = [tile - step * tile[k:k + 1] for tile in tiles]
    scales = 1.0 / jnp.sqrt(scales)
    return jnp.concatenate([tile * scales for tile in tiles], axis=1)


def mnf_kernel(signal_scale, noise_scale, kept, signal_ref, noise_ref, filter_ref, work):
    size = signal_ref.shape[0]
    wide = work.shape[1] // 3
    work[...] = jnp.zeros_like(work)
    work[:, :size] = noise_ref[...] * noise_scale
    ids = lax.broadcasted_iota(jnp.int32, (size, size), 0)
    work[:, wide:wide + size] = jnp.where(
        ids == lax.broadcasted_iota(jnp.int32, (size, size), 1), 1.0, 0.0
    )
    work[:, 2 * wide:2 * wide + size] = signal_ref[...] * signal_scale
    for start in range(0, size, PANEL):
        end = min(start + PANEL, size)
        rows = eliminate(work[start:end, :], start)
        work[start:end, :] = rows
        if end < size:
            step = contract(rows[:, end:size], rows, 0, 0)
            work[end:, :] = work[end:, :] - step
    upper = work[:, :wide]
    upper = jnp.where(
        lax.broadcasted_iota(jnp.int32, (size, wide), 1)
        >= lax.broadcasted_iota(jnp.int32, (size, wide), 0),
        upper, 0.0,
    )
    inverse = work[:, wide:2 * wide]
    half_solved = work[:, 2 * wide:]
    margin = jnp.zeros((wide - size, wide), jnp.float32)
    inner = contract(
        jnp.concatenate([half_solved, margin], axis=0),
        jnp.concatenate([inverse, margin], axis=0), 1, 1,
    )
    whitened = 0.5 * (inner + inner.T)
    mapped = whitened[:kept]
    for iteration in range(ITERS):
        if iteration:
            mapped = contract(mapped, whitened, 1, 0)
        gram = contract(mapped, mapped, 1, 1)
        gram = jnp.concatenate([gram, jnp.zeros((kept, 128 - kept), jnp.float32)], axis=1)
        mapped = eliminate(jnp.concatenate([gram, mapped], axis=1), 0)[:, 128:]
    subspace = mapped[:, :size]
    forward = contract(subspace, inverse, 1, 0)
    backward = contract(subspace, upper, 1, 0)
    filter_ref[...] = contract(forward, backward, 0, 0)[:size, :size]


def mnf_filter(signal_total, noise_total, signal_count, noise_count, kept):
    size = signal_total.shape[0]
    wide = -(-size // 128) * 128
    kernel = functools.partial(mnf_kernel, 1.0 / signal_count, 1.0 / noise_count, kept)
    return pl.pallas_call(
        kernel,
        out_shape=jax.ShapeDtypeStruct((size, size), jnp.float32),
        in_specs=[pl.BlockSpec(memory_space=pltpu.VMEM)] * 2,
        out_specs=pl.BlockSpec(memory_space=pltpu.VMEM),
        scratch_shapes=[pltpu.VMEM((size, 3 * wide), jnp.float32)],
        name="mnf_filter",
    )(signal_total, noise_total)


def body(radiance):
    local_block = radiance[0]
    row_count = local_block.shape[0]
    column_count = local_block.shape[2]
    track_count = lax.axis_size("track")
    line_count = lax.axis_size("line")
    total_rows = row_count * track_count
    values = local_block.astype(jnp.float32)
    first_sum = jnp.sum(values, axis=0)
    second_sum = jnp.sum(values * values, axis=0)
    first_total, second_total = lax.psum((first_sum, second_sum), "track")
    col_mean, factor, band_mean = column_terms(first_total, second_total, total_rows)
    centred = ((values - col_mean) * factor).astype(jnp.bfloat16)
    following = from_behind(centred[:1], "track", -1)
    rows_ahead = jnp.concatenate([centred[1:], following], axis=0)
    keep_last = lax.axis_index("track") < track_count - 1
    row_index = jnp.arange(row_count)
    row_keep = jnp.where((row_index < row_count - 1) | keep_last, 1.0, 0.0).astype(jnp.float32)
    differences = (
        (rows_ahead.astype(jnp.float32) - centred.astype(jnp.float32)) * row_keep[:, None, None]
    ).astype(jnp.bfloat16)
    signal_part = jnp.einsum("rbc,rdc->bd", centred, centred, preferred_element_type=jnp.float32)
    noise_part = jnp.einsum(
        "rbc,rdc->bd", differences, differences, preferred_element_type=jnp.float32
    )
    signal_total, noise_total = lax.psum((signal_part, noise_part), ("line", "track"))
    signal_count = line_count * total_rows * column_count
    noise_count = 2 * line_count * (total_rows - 1) * column_count
    filter_matrix = mnf_filter(signal_total, noise_total, signal_count, noise_count, NCOMP)
    narrow = filter_matrix.astype(jnp.bfloat16)
    mixed = jnp.einsum("ab,rac->rbc", narrow, centred, preferred_element_type=jnp.float32)
    cleaned = (band_mean[:, None] + mixed).astype(jnp.bfloat16)
    return (cleaned[None], filter_matrix)


def solution(mesh):
    in_specs = (P("line", "track", None, None),)
    out_specs = (P("line", "track", None, None), P())
    return jax.shard_map(body, mesh=mesh, in_specs=in_specs, out_specs=out_specs, check_vma=False)
```

```python
import functools

import jax
import jax.numpy as jnp
from jax import lax
from jax.experimental import pallas as pl
from jax.experimental.pallas import tpu as pltpu
from jax.sharding import PartitionSpec as P

NCOMP = 40
ITERS = 4


EPSILON = 1e-05
HIGHEST = lax.Precision.HIGHEST


def from_behind(block, axis, distance):
    devices = range(lax.axis_size(axis))
    route = [(i - distance, i) for i in devices if i - distance in devices]
    return lax.ppermute(block, axis, route)


def column_terms(first_total, second_total, total_rows):
    col_mean = first_total / total_rows
    col_spread = jnp.sqrt(second_total / total_rows - col_mean * col_mean + EPSILON)
    band_mean = jnp.mean(col_mean, axis=1)
    factor = jnp.mean(col_spread, axis=1)[:, None] / col_spread
    return (col_mean, factor, band_mean)


PANEL = 32
GROUP = 8


def contract(left, right, left_axis, right_axis):
    return lax.dot_general(
        left, right, (((left_axis,), (right_axis,)), ((), ())),
        precision=HIGHEST, preferred_element_type=jnp.float32,
    )


def eliminate(panel, offset):
    size = panel.shape[0]
    row_ids = lax.broadcasted_iota(jnp.int32, (size, 128), 0)
    repeats = panel.shape[1] // 128
    tiles = [panel[:, t * 128:(t + 1) * 128] for t in range(repeats)]
    home, shift = divmod(offset, 128)
    scales = jnp.zeros((size, 128), jnp.float32)
    for start in range(0, size, GROUP):
        lanes = range(start, min(start + GROUP, size))
        columns = {}
        for k in lanes:
            tile, lane = divmod(offset + k, 128)
            columns[k] = jnp.broadcast_to(tiles[tile][:, lane:lane + 1], (size, 128))
        for k in lanes:
            pivot_row = jnp.broadcast_to(columns[k][k:k + 1], (size, 128))
            scales = jnp.where(row_ids == k, pivot_row, scales)
            step = jnp.where(row_ids > k, columns[k] * (1.0 / pivot_row), 0.0)
            for later in lanes:
                if later > k:
                    columns[later] = columns[later] - step * columns[later][k:k + 1]
            tiles = [tile - step * tile[k:k + 1] for tile in tiles]
    scales = 1.0 / jnp.sqrt(scales)
    return jnp.concatenate([tile * scales for tile in tiles], axis=1)


def mnf_kernel(signal_scale, noise_scale, kept, packed_ref, filter_ref, work):
    size = filter_ref.shape[0]
    wide = packed_ref.shape[0]
    packed = packed_ref[...]
    row_ids = lax.broadcasted_iota(jnp.int32, (wide, wide), 0)
    column_ids = lax.broadcasted_iota(jnp.int32, (wide, wide), 1)
    below = jnp.where((row_ids > column_ids) & (row_ids < size), packed, 0.0)
    above = jnp.where(row_ids < column_ids, packed, 0.0)
    diagonal = row_ids == column_ids
    noise = below + below.T + jnp.where(diagonal, packed, 0.0)
    signal = above + above.T + jnp.where(diagonal, packed[size:size + 1], 0.0)
    work[:, :wide] = noise[:size] * noise_scale
    work[:, wide:2 * wide] = jnp.where(diagonal, 1.0, 0.0)[:size]
    work[:, 2 * wide:] = signal[:size] * signal_scale
    for start in range(0, size, PANEL):
        end = min(start + PANEL, size)
        rows = eliminate(work[start:end, :], start)
        work[start:end, :] = rows
        if end < size:
            step = contract(rows[:, end:size], rows, 0, 0)
            work[end:, :] = work[end:, :] - step
    upper = work[:, :wide]
    upper = jnp.where(
        lax.broadcasted_iota(jnp.int32, (size, wide), 1)
        >= lax.broadcasted_iota(jnp.int32, (size, wide), 0),
        upper, 0.0,
    )
    inverse = work[:, wide:2 * wide]
    half_solved = work[:, 2 * wide:]
    margin = jnp.zeros((wide - size, wide), jnp.float32)
    inner = contract(
        jnp.concatenate([half_solved, margin], axis=0),
        jnp.concatenate([inverse, margin], axis=0), 1, 1,
    )
    whitened = 0.5 * (inner + inner.T)
    mapped = whitened[:kept]
    for iteration in range(ITERS):
        if iteration:
            mapped = contract(mapped, whitened, 1, 0)
        gram = contract(mapped, mapped, 1, 1)
        gram = jnp.concatenate([gram, jnp.zeros((kept, 128 - kept), jnp.float32)], axis=1)
        mapped = eliminate(jnp.concatenate([gram, mapped], axis=1), 0)[:, 128:]
    subspace = mapped[:, :size]
    forward = contract(subspace, inverse, 1, 0)
    backward = contract(subspace, upper, 1, 0)
    filter_ref[...] = contract(forward, backward, 0, 0)[:size, :size]


def mnf_filter(packed, size, signal_count, noise_count, kept):
    wide = packed.shape[0]
    return pl.pallas_call(
        functools.partial(mnf_kernel, 1.0 / signal_count, 1.0 / noise_count, kept),
        out_shape=jax.ShapeDtypeStruct((size, size), jnp.float32),
        in_specs=[pl.BlockSpec(memory_space=pltpu.VMEM)],
        out_specs=pl.BlockSpec(memory_space=pltpu.VMEM),
        scratch_shapes=[pltpu.VMEM((size, 3 * wide), jnp.float32)],
        name="mnf_filter",
    )(packed)


def track_place(track):
    return (lax.axis_index("line"), track)


def stats_kernel(tracks, x_ref, out_ref, paired, mine, slots, gathered, other, send, recv):
    chips = tracks // 2
    half = x_ref.shape[1] // 2
    width = x_ref.shape[2] // chips
    track = lax.axis_index("track")
    core, chip = lax.rem(track, 2), lax.div(track, 2)
    partner = track_place(chip * 2 + 1 - core)
    own_rows = pl.ds(pl.multiple_of(core * half, 8), half)
    other_rows = pl.ds(pl.multiple_of((1 - core) * half, 8), half)

    def ahead(step):
        q = lax.rem(chip + step, chips)
        return q, track_place(q * 2 + core), pl.ds(pl.multiple_of(q * width, 128), width)

    def copy(source, target, phase, sent, landed, device):
        return pltpu.make_async_remote_copy(
            src_ref=source, dst_ref=target, send_sem=send.at[phase, sent],
            recv_sem=recv.at[phase, landed], device_id=device,
            device_id_type=pl.DeviceIdType.MESH,
        )

    barrier = pltpu.get_barrier_semaphore()
    pl.semaphore_signal(barrier, inc=1, device_id=partner, device_id_type=pl.DeviceIdType.MESH)
    for step in range(1, chips):
        pl.semaphore_signal(
            barrier, inc=1, device_id=ahead(step)[1], device_id_type=pl.DeviceIdType.MESH
        )
    pl.semaphore_wait(barrier, chips)

    started = []
    for step in range(1, chips + 1):
        q, _, lanes = ahead(step)
        pair = copy(x_ref.at[:, other_rows, lanes], paired.at[q], 0, q, q, partner)
        pair.start()
        started.append(pair)
    for step in range(1, chips + 1):
        q, peer, lanes = ahead(step)
        started[step - 1].wait_recv()
        mine[q] = x_ref[:, own_rows, lanes] + paired[q]
        if step < chips:
            scatter = copy(mine.at[q], slots.at[chip], 1, q, chip, peer)
            scatter.start()
            started.append(scatter)
    total = mine[chip]
    for step in range(1, chips):
        q, peer, _ = ahead(chips - step)
        copy(mine.at[q], slots.at[q], 1, q, q, peer).wait_recv()
        total = total + slots[q]
    gathered[chip] = total
    for step in range(1, chips):
        q, peer, _ = ahead(step)
        gather = copy(gathered.at[chip], gathered.at[chip], 2, q, chip, peer)
        gather.start()
        started.append(gather)
    forward = copy(gathered.at[chip], other.at[chip], 3, chip, chip, partner)
    forward.start()
    started.append(forward)
    for step in range(1, chips):
        q, peer, _ = ahead(chips - step)
        copy(gathered.at[q], gathered.at[q], 2, q, q, peer).wait_recv()
        forward = copy(gathered.at[q], other.at[q], 3, q, q, partner)
        forward.start()
        started.append(forward)
    for q in range(chips):
        out_ref[:, own_rows, q * width:(q + 1) * width] = gathered[q]
    for q in range(chips):
        copy(other.at[q], other.at[q], 3, q, q, partner).wait_recv()
        out_ref[:, other_rows, q * width:(q + 1) * width] = other[q]
    for item in started:
        item.wait_send()


def stats_total(sums, tracks):
    chips = tracks // 2
    _, bands, lanes = sums.shape
    piece = (chips, 2, bands // 2, lanes // chips)
    return pl.pallas_call(
        functools.partial(stats_kernel, tracks),
        out_shape=jax.ShapeDtypeStruct(sums.shape, jnp.float32),
        in_specs=[pl.BlockSpec(memory_space=pltpu.VMEM)],
        out_specs=pl.BlockSpec(memory_space=pltpu.VMEM),
        scratch_shapes=[pltpu.VMEM(piece, jnp.float32)] * 5
        + [pltpu.SemaphoreType.DMA((4, chips))] * 2,
        compiler_params=pltpu.CompilerParams(collective_id=1, has_side_effects=True),
        name="stats_total",
    )(sums)


def gram_kernel(lines, tracks, x_ref, out_ref, slots, full, send, recv):
    count = lines * tracks
    me = lax.axis_index("line") * tracks + lax.axis_index("track")

    def ahead(step):
        peer = lax.rem(me + step, count)
        return peer, (lax.div(peer, tracks), lax.rem(peer, tracks))

    def settle(ref, sem):
        everyone = ref.at[pl.ds(0, count - 1)]
        pltpu.make_async_copy(everyone, everyone, sem).wait()

    barrier = pltpu.get_barrier_semaphore()

    @pl.loop(1, count)
    def _(step):
        pl.semaphore_signal(
            barrier, inc=1, device_id=ahead(step)[1], device_id_type=pl.DeviceIdType.MESH
        )

    pl.semaphore_wait(barrier, count - 1)

    @pl.loop(1, count)
    def _(step):
        peer, place = ahead(step)
        pltpu.make_async_remote_copy(
            src_ref=x_ref.at[peer], dst_ref=slots.at[me], send_sem=send.at[0],
            recv_sem=recv.at[0], device_id=place, device_id_type=pl.DeviceIdType.MESH,
        ).start()

    slots[me] = x_ref[me]
    settle(slots, recv.at[0])
    full[me] = jnp.sum(slots[...], axis=0)

    @pl.loop(1, count)
    def _(step):
        pltpu.make_async_remote_copy(
            src_ref=full.at[me], dst_ref=full.at[me], send_sem=send.at[1],
            recv_sem=recv.at[1], device_id=ahead(step)[1],
            device_id_type=pl.DeviceIdType.MESH,
        ).start()

    settle(full, recv.at[1])
    out_ref[...] = full[...]
    settle(x_ref, send.at[0])
    settle(full, send.at[1])


def gram_total(packed, lines, tracks):
    count = lines * tracks
    height, wide = packed.shape
    rows = -(-height // (8 * count)) * 8
    padded = jnp.pad(packed, ((0, count * rows - height), (0, 0)))
    piece = (count, rows, wide)
    total = pl.pallas_call(
        functools.partial(gram_kernel, lines, tracks),
        out_shape=jax.ShapeDtypeStruct(piece, jnp.float32),
        in_specs=[pl.BlockSpec(memory_space=pltpu.VMEM)],
        out_specs=pl.BlockSpec(memory_space=pltpu.VMEM),
        scratch_shapes=[pltpu.VMEM(piece, jnp.float32)] * 2
        + [pltpu.SemaphoreType.DMA((2,))] * 2,
        compiler_params=pltpu.CompilerParams(collective_id=0, has_side_effects=True),
        name="gram_total",
    )(padded.reshape(piece))
    return total.reshape(count * rows, wide)[:height]


def pack_grams(signal_part, noise_part, wide):
    size = signal_part.shape[0]
    above = jnp.arange(size)[:, None] < jnp.arange(size)[None, :]
    square = jnp.where(above, signal_part, noise_part)
    packed = jnp.concatenate([square, jnp.diagonal(signal_part)[None]], axis=0)
    return jnp.pad(packed, ((0, wide - size - 1), (0, wide - size)))


def body(radiance):
    local_block = radiance[0]
    row_count = local_block.shape[0]
    column_count = local_block.shape[2]
    track_count = lax.axis_size("track")
    line_count = lax.axis_size("line")
    total_rows = row_count * track_count
    values = local_block.astype(jnp.float32)
    sums = jnp.stack([jnp.sum(values, axis=0), jnp.sum(values * values, axis=0)])
    strip = 128 * (track_count // 2)
    margin = -column_count % strip
    totals = stats_total(jnp.pad(sums, ((0, 0), (0, 0), (0, margin))), track_count)
    first_total, second_total = totals[0, :, :column_count], totals[1, :, :column_count]
    col_mean, factor, band_mean = column_terms(first_total, second_total, total_rows)
    centred = ((values - col_mean) * factor).astype(jnp.bfloat16)
    following = from_behind(centred[:1], "track", -1)
    rows_ahead = jnp.concatenate([centred[1:], following], axis=0)
    keep_last = lax.axis_index("track") < track_count - 1
    row_index = jnp.arange(row_count)
    row_keep = jnp.where((row_index < row_count - 1) | keep_last, 1.0, 0.0).astype(jnp.float32)
    differences = (
        (rows_ahead.astype(jnp.float32) - centred.astype(jnp.float32)) * row_keep[:, None, None]
    ).astype(jnp.bfloat16)
    signal_part = jnp.einsum("rbc,rdc->bd", centred, centred, preferred_element_type=jnp.float32)
    noise_part = jnp.einsum(
        "rbc,rdc->bd", differences, differences, preferred_element_type=jnp.float32
    )
    size = signal_part.shape[0]
    wide = (size // 128 + 1) * 128
    packed = gram_total(pack_grams(signal_part, noise_part, wide), line_count, track_count)
    signal_count = line_count * total_rows * column_count
    noise_count = 2 * line_count * (total_rows - 1) * column_count
    filter_matrix = mnf_filter(packed, size, signal_count, noise_count, NCOMP)
    narrow = filter_matrix.astype(jnp.bfloat16)
    mixed = jnp.einsum("ab,rac->rbc", narrow, centred, preferred_element_type=jnp.float32)
    cleaned = (band_mean[:, None] + mixed).astype(jnp.bfloat16)
    return (cleaned[None], filter_matrix)


def solution(mesh):
    in_specs = (P("line", "track", None, None),)
    out_specs = (P("line", "track", None, None), P())
    return jax.shard_map(body, mesh=mesh, in_specs=in_specs, out_specs=out_specs, check_vma=False)
```

```python
import functools

import jax
import jax.numpy as jnp
from jax import lax
from jax.experimental import pallas as pl
from jax.experimental.pallas import tpu as pltpu
from jax.sharding import PartitionSpec as P

NCOMP = 40
ITERS = 4


EPSILON = 1e-05
HIGHEST = lax.Precision.HIGHEST


def from_behind(block, axis, distance):
    devices = range(lax.axis_size(axis))
    route = [(i - distance, i) for i in devices if i - distance in devices]
    return lax.ppermute(block, axis, route)


def column_terms(first_total, second_total, total_rows):
    col_mean = first_total / total_rows
    col_spread = jnp.sqrt(second_total / total_rows - col_mean * col_mean + EPSILON)
    band_mean = jnp.mean(col_mean, axis=1)
    factor = jnp.mean(col_spread, axis=1)[:, None] / col_spread
    return (col_mean, factor, band_mean)


PANEL = 32
GROUP = 8


def contract(left, right, left_axis, right_axis):
    return lax.dot_general(
        left, right, (((left_axis,), (right_axis,)), ((), ())),
        precision=HIGHEST, preferred_element_type=jnp.float32,
    )


def eliminate(panel, offset):
    size = panel.shape[0]
    row_ids = lax.broadcasted_iota(jnp.int32, (size, 128), 0)
    repeats = panel.shape[1] // 128
    tiles = [panel[:, t * 128:(t + 1) * 128] for t in range(repeats)]
    home, shift = divmod(offset, 128)
    scales = jnp.zeros((size, 128), jnp.float32)
    for start in range(0, size, GROUP):
        lanes = range(start, min(start + GROUP, size))
        columns = {}
        for k in lanes:
            tile, lane = divmod(offset + k, 128)
            columns[k] = jnp.broadcast_to(tiles[tile][:, lane:lane + 1], (size, 128))
        for k in lanes:
            pivot_row = jnp.broadcast_to(columns[k][k:k + 1], (size, 128))
            scales = jnp.where(row_ids == k, pivot_row, scales)
            step = jnp.where(row_ids > k, columns[k] * (1.0 / pivot_row), 0.0)
            for later in lanes:
                if later > k:
                    columns[later] = columns[later] - step * columns[later][k:k + 1]
            tiles = [tile - step * tile[k:k + 1] for tile in tiles]
    scales = 1.0 / jnp.sqrt(scales)
    return jnp.concatenate([tile * scales for tile in tiles], axis=1)


def mnf_kernel(signal_scale, noise_scale, kept, packed_ref, filter_ref, work):
    size = filter_ref.shape[0]
    wide = packed_ref.shape[0]
    packed = packed_ref[...]
    row_ids = lax.broadcasted_iota(jnp.int32, (wide, wide), 0)
    column_ids = lax.broadcasted_iota(jnp.int32, (wide, wide), 1)
    below = jnp.where((row_ids > column_ids) & (row_ids < size), packed, 0.0)
    above = jnp.where(row_ids < column_ids, packed, 0.0)
    diagonal = row_ids == column_ids
    noise = below + below.T + jnp.where(diagonal, packed, 0.0)
    signal = above + above.T + jnp.where(diagonal, packed[size:size + 1], 0.0)
    work[:, :wide] = noise[:size] * noise_scale
    work[:, wide:2 * wide] = jnp.where(diagonal, 1.0, 0.0)[:size]
    work[:, 2 * wide:] = signal[:size] * signal_scale
    for start in range(0, size, PANEL):
        end = min(start + PANEL, size)
        rows = eliminate(work[start:end, :], start)
        work[start:end, :] = rows
        if end < size:
            step = contract(rows[:, end:size], rows, 0, 0)
            work[end:, :] = work[end:, :] - step
    upper = work[:, :wide]
    upper = jnp.where(
        lax.broadcasted_iota(jnp.int32, (size, wide), 1)
        >= lax.broadcasted_iota(jnp.int32, (size, wide), 0),
        upper, 0.0,
    )
    inverse = work[:, wide:2 * wide]
    half_solved = work[:, 2 * wide:]
    margin = jnp.zeros((wide - size, wide), jnp.float32)
    inner = contract(
        jnp.concatenate([half_solved, margin], axis=0),
        jnp.concatenate([inverse, margin], axis=0), 1, 1,
    )
    whitened = 0.5 * (inner + inner.T)
    mapped = whitened[:kept]
    for iteration in range(ITERS):
        if iteration:
            mapped = contract(mapped, whitened, 1, 0)
        gram = contract(mapped, mapped, 1, 1)
        gram = jnp.concatenate([gram, jnp.zeros((kept, 128 - kept), jnp.float32)], axis=1)
        mapped = eliminate(jnp.concatenate([gram, mapped], axis=1), 0)[:, 128:]
    subspace = mapped[:, :size]
    forward = contract(subspace, inverse, 1, 0)
    backward = contract(subspace, upper, 1, 0)
    filter_ref[...] = contract(forward, backward, 0, 0)[:size, :size]


def mnf_filter(packed, size, signal_count, noise_count, kept):
    wide = packed.shape[0]
    return pl.pallas_call(
        functools.partial(mnf_kernel, 1.0 / signal_count, 1.0 / noise_count, kept),
        out_shape=jax.ShapeDtypeStruct((size, size), jnp.float32),
        in_specs=[pl.BlockSpec(memory_space=pltpu.VMEM)],
        out_specs=pl.BlockSpec(memory_space=pltpu.VMEM),
        scratch_shapes=[pltpu.VMEM((size, 3 * wide), jnp.float32)],
        name="mnf_filter",
    )(packed)


def track_place(track):
    return (lax.axis_index("line"), track)


def stats_kernel(tracks, x_ref, out_ref, paired, mine, slots, gathered, other, send, recv):
    chips = tracks // 2
    half = x_ref.shape[1] // 2
    width = x_ref.shape[2] // chips
    track = lax.axis_index("track")
    core, chip = lax.rem(track, 2), lax.div(track, 2)
    partner = track_place(chip * 2 + 1 - core)
    own_rows = pl.ds(pl.multiple_of(core * half, 8), half)
    other_rows = pl.ds(pl.multiple_of((1 - core) * half, 8), half)

    def ahead(step):
        q = lax.rem(chip + step, chips)
        return q, track_place(q * 2 + core), pl.ds(pl.multiple_of(q * width, 128), width)

    def copy(source, target, phase, sent, landed, device):
        return pltpu.make_async_remote_copy(
            src_ref=source, dst_ref=target, send_sem=send.at[phase, sent],
            recv_sem=recv.at[phase, landed], device_id=device,
            device_id_type=pl.DeviceIdType.MESH,
        )

    barrier = pltpu.get_barrier_semaphore()
    pl.semaphore_signal(barrier, inc=1, device_id=partner, device_id_type=pl.DeviceIdType.MESH)
    for step in range(1, chips):
        pl.semaphore_signal(
            barrier, inc=1, device_id=ahead(step)[1], device_id_type=pl.DeviceIdType.MESH
        )
    pl.semaphore_wait(barrier, chips)

    started = []
    for step in range(1, chips + 1):
        q, _, lanes = ahead(step)
        pair = copy(x_ref.at[:, other_rows, lanes], paired.at[q], 0, q, q, partner)
        pair.start()
        started.append(pair)
    for step in range(1, chips + 1):
        q, peer, lanes = ahead(step)
        started[step - 1].wait_recv()
        mine[q] = x_ref[:, own_rows, lanes] + paired[q]
        if step < chips:
            scatter = copy(mine.at[q], slots.at[chip], 1, q, chip, peer)
            scatter.start()
            started.append(scatter)
    total = mine[chip]
    for step in range(1, chips):
        q, peer, _ = ahead(chips - step)
        copy(mine.at[q], slots.at[q], 1, q, q, peer).wait_recv()
        total = total + slots[q]
    gathered[chip] = total
    for step in range(1, chips):
        q, peer, _ = ahead(step)
        gather = copy(gathered.at[chip], gathered.at[chip], 2, q, chip, peer)
        gather.start()
        started.append(gather)
    forward = copy(gathered.at[chip], other.at[chip], 3, chip, chip, partner)
    forward.start()
    started.append(forward)
    for step in range(1, chips):
        q, peer, _ = ahead(chips - step)
        copy(gathered.at[q], gathered.at[q], 2, q, q, peer).wait_recv()
        forward = copy(gathered.at[q], other.at[q], 3, q, q, partner)
        forward.start()
        started.append(forward)
    for q in range(chips):
        out_ref[:, own_rows, q * width:(q + 1) * width] = gathered[q]
    for q in range(chips):
        copy(other.at[q], other.at[q], 3, q, q, partner).wait_recv()
        out_ref[:, other_rows, q * width:(q + 1) * width] = other[q]
    for item in started:
        item.wait_send()


def stats_total(sums, tracks):
    chips = tracks // 2
    _, bands, lanes = sums.shape
    piece = (chips, 2, bands // 2, lanes // chips)
    return pl.pallas_call(
        functools.partial(stats_kernel, tracks),
        out_shape=jax.ShapeDtypeStruct(sums.shape, jnp.float32),
        in_specs=[pl.BlockSpec(memory_space=pltpu.VMEM)],
        out_specs=pl.BlockSpec(memory_space=pltpu.VMEM),
        scratch_shapes=[pltpu.VMEM(piece, jnp.float32)] * 5
        + [pltpu.SemaphoreType.DMA((4, chips))] * 2,
        compiler_params=pltpu.CompilerParams(collective_id=1, has_side_effects=True),
        name="stats_total",
    )(sums)


def gram_kernel(lines, chips, x_ref, out_ref, paired, by_line, by_chip, half, quarter, full, send, recv):
    line = lax.axis_index("line")
    track = lax.axis_index("track")
    core, chip = lax.rem(track, 2), lax.div(track, 2)
    partner = (line, chip * 2 + 1 - core)
    other_lines = [(q, (q, track)) for q in (lax.rem(line + s, lines) for s in range(1, lines))]
    other_chips = [
        (q, (line, q * 2 + core)) for q in (lax.rem(chip + s, chips) for s in range(1, chips))
    ]
    started = []

    def copy(source, target, phase, sent, landed, device):
        return pltpu.make_async_remote_copy(
            src_ref=source, dst_ref=target, send_sem=send.at[phase, sent],
            recv_sem=recv.at[phase, landed], device_id=device,
            device_id_type=pl.DeviceIdType.MESH,
        )

    def launch(*args):
        item = copy(*args)
        item.start()
        started.append(item)

    barrier = pltpu.get_barrier_semaphore()
    for place in [partner] + [place for _, place in other_lines + other_chips]:
        pl.semaphore_signal(barrier, inc=1, device_id=place, device_id_type=pl.DeviceIdType.MESH)
    pl.semaphore_wait(barrier, lines + chips - 1)

    launch(x_ref.at[1 - core], paired, 0, 0, 0, partner)
    copy(paired, paired, 0, 0, 0, partner).wait_recv()
    half[...] = x_ref[core] + paired[...]
    for q, place in other_lines:
        launch(half.at[q], by_line.at[line], 1, q, line, place)
    part = half[line]
    for q, place in other_lines:
        copy(by_line.at[q], by_line.at[q], 1, q, q, place).wait_recv()
        part = part + by_line[q]
    quarter[...] = part
    for q, place in other_chips:
        launch(quarter.at[q], by_chip.at[chip], 2, q, chip, place)
    total = quarter[chip]
    for q, place in other_chips[::-1]:
        copy(by_chip.at[q], by_chip.at[q], 2, q, q, place).wait_recv()
        total = total + by_chip[q]
    full[core, line, chip] = total
    own = full.at[core, line, chip]
    for q, place in other_chips:
        launch(own, own, 3, q, chip, place)
    for q, place in other_chips[::-1]:
        copy(full.at[core, line, q], full.at[core, line, q], 3, q, q, place).wait_recv()
    own = full.at[core, line]
    for q, place in other_lines:
        launch(own, own, 4, q, line, place)
    for q, place in other_lines:
        copy(full.at[core, q], full.at[core, q], 4, q, q, place).wait_recv()
    own = full.at[core]
    launch(own, own, 5, 0, 0, partner)
    copy(full.at[1 - core], full.at[1 - core], 5, 0, 0, partner).wait_recv()
    out_ref[...] = full[...]
    for item in started:
        item.wait_send()


def gram_total(packed, lines, tracks):
    chips = tracks // 2
    count = lines * tracks
    height, wide = packed.shape
    rows = -(-height // (8 * count)) * 8
    padded = jnp.pad(packed, ((0, count * rows - height), (0, 0)))
    piece = (rows, wide)
    whole = (2, lines, chips) + piece
    shapes = [(lines, chips) + piece, (lines, chips) + piece, (chips,) + piece,
              (lines, chips) + piece, (chips,) + piece, whole]
    total = pl.pallas_call(
        functools.partial(gram_kernel, lines, chips),
        out_shape=jax.ShapeDtypeStruct(whole, jnp.float32),
        in_specs=[pl.BlockSpec(memory_space=pltpu.VMEM)],
        out_specs=pl.BlockSpec(memory_space=pltpu.VMEM),
        scratch_shapes=[pltpu.VMEM(shape, jnp.float32) for shape in shapes]
        + [pltpu.SemaphoreType.DMA((6, max(lines, chips)))] * 2,
        compiler_params=pltpu.CompilerParams(collective_id=0, has_side_effects=True),
        name="gram_total",
    )(padded.reshape(whole))
    return total.reshape(count * rows, wide)[:height]


def pack_grams(signal_part, noise_part, wide):
    size = signal_part.shape[0]
    above = jnp.arange(size)[:, None] < jnp.arange(size)[None, :]
    square = jnp.where(above, signal_part, noise_part)
    packed = jnp.concatenate([square, jnp.diagonal(signal_part)[None]], axis=0)
    return jnp.pad(packed, ((0, wide - size - 1), (0, wide - size)))


def body(radiance):
    local_block = radiance[0]
    row_count = local_block.shape[0]
    column_count = local_block.shape[2]
    track_count = lax.axis_size("track")
    line_count = lax.axis_size("line")
    total_rows = row_count * track_count
    values = local_block.astype(jnp.float32)
    sums = jnp.stack([jnp.sum(values, axis=0), jnp.sum(values * values, axis=0)])
    strip = 128 * (track_count // 2)
    margin = -column_count % strip
    totals = stats_total(jnp.pad(sums, ((0, 0), (0, 0), (0, margin))), track_count)
    first_total, second_total = totals[0, :, :column_count], totals[1, :, :column_count]
    col_mean, factor, band_mean = column_terms(first_total, second_total, total_rows)
    centred = ((values - col_mean) * factor).astype(jnp.bfloat16)
    following = from_behind(centred[:1], "track", -1)
    rows_ahead = jnp.concatenate([centred[1:], following], axis=0)
    keep_last = lax.axis_index("track") < track_count - 1
    row_index = jnp.arange(row_count)
    row_keep = jnp.where((row_index < row_count - 1) | keep_last, 1.0, 0.0).astype(jnp.float32)
    differences = (
        (rows_ahead.astype(jnp.float32) - centred.astype(jnp.float32)) * row_keep[:, None, None]
    ).astype(jnp.bfloat16)
    signal_part = jnp.einsum("rbc,rdc->bd", centred, centred, preferred_element_type=jnp.float32)
    noise_part = jnp.einsum(
        "rbc,rdc->bd", differences, differences, preferred_element_type=jnp.float32
    )
    size = signal_part.shape[0]
    wide = (size // 128 + 1) * 128
    packed = gram_total(pack_grams(signal_part, noise_part, wide), line_count, track_count)
    signal_count = line_count * total_rows * column_count
    noise_count = 2 * line_count * (total_rows - 1) * column_count
    filter_matrix = mnf_filter(packed, size, signal_count, noise_count, NCOMP)
    narrow = filter_matrix.astype(jnp.bfloat16)
    mixed = jnp.einsum("ab,rac->rbc", narrow, centred, preferred_element_type=jnp.float32)
    cleaned = (band_mean[:, None] + mixed).astype(jnp.bfloat16)
    return (cleaned[None], filter_matrix)


def solution(mesh):
    in_specs = (P("line", "track", None, None),)
    out_specs = (P("line", "track", None, None), P())
    return jax.shard_map(body, mesh=mesh, in_specs=in_specs, out_specs=out_specs, check_vma=False)
```

```python
import functools

import jax
import jax.numpy as jnp
from jax import lax
from jax.experimental import pallas as pl
from jax.experimental.pallas import tpu as pltpu
from jax.sharding import PartitionSpec as P

NCOMP = 40
ITERS = 4


EPSILON = 1e-05
HIGHEST = lax.Precision.HIGHEST


def from_behind(block, axis, distance):
    devices = range(lax.axis_size(axis))
    route = [(i - distance, i) for i in devices if i - distance in devices]
    return lax.ppermute(block, axis, route)


def column_terms(first_total, second_total, total_rows):
    col_mean = first_total / total_rows
    col_spread = jnp.sqrt(second_total / total_rows - col_mean * col_mean + EPSILON)
    band_mean = jnp.mean(col_mean, axis=1)
    factor = jnp.mean(col_spread, axis=1)[:, None] / col_spread
    return (col_mean, factor, band_mean)


PANEL = 32
GROUP = 8


def contract(left, right, left_axis, right_axis):
    return lax.dot_general(
        left, right, (((left_axis,), (right_axis,)), ((), ())),
        precision=HIGHEST, preferred_element_type=jnp.float32,
    )


def eliminate(panel, offset):
    size = panel.shape[0]
    row_ids = lax.broadcasted_iota(jnp.int32, (size, 128), 0)
    repeats = panel.shape[1] // 128
    tiles = [panel[:, t * 128:(t + 1) * 128] for t in range(repeats)]
    home, shift = divmod(offset, 128)
    scales = jnp.zeros((size, 128), jnp.float32)
    for start in range(0, size, GROUP):
        lanes = range(start, min(start + GROUP, size))
        columns = {}
        for k in lanes:
            tile, lane = divmod(offset + k, 128)
            columns[k] = jnp.broadcast_to(tiles[tile][:, lane:lane + 1], (size, 128))
        for k in lanes:
            pivot_row = jnp.broadcast_to(columns[k][k:k + 1], (size, 128))
            scales = jnp.where(row_ids == k, pivot_row, scales)
            step = jnp.where(row_ids > k, columns[k] * (1.0 / pivot_row), 0.0)
            for later in lanes:
                if later > k:
                    columns[later] = columns[later] - step * columns[later][k:k + 1]
            tiles = [tile - step * tile[k:k + 1] for tile in tiles]
    scales = 1.0 / jnp.sqrt(scales)
    return jnp.concatenate([tile * scales for tile in tiles], axis=1)


def mnf_kernel(signal_scale, noise_scale, kept, packed_ref, filter_ref, work):
    size = filter_ref.shape[0]
    wide = packed_ref.shape[0]
    packed = packed_ref[...]
    row_ids = lax.broadcasted_iota(jnp.int32, (wide, wide), 0)
    column_ids = lax.broadcasted_iota(jnp.int32, (wide, wide), 1)
    below = jnp.where((row_ids > column_ids) & (row_ids < size), packed, 0.0)
    above = jnp.where(row_ids < column_ids, packed, 0.0)
    diagonal = row_ids == column_ids
    noise = below + below.T + jnp.where(diagonal, packed, 0.0)
    signal = above + above.T + jnp.where(diagonal, packed[size:size + 1], 0.0)
    work[:, :wide] = noise[:size] * noise_scale
    work[:, wide:2 * wide] = jnp.where(diagonal, 1.0, 0.0)[:size]
    work[:, 2 * wide:] = signal[:size] * signal_scale
    for start in range(0, size, PANEL):
        end = min(start + PANEL, size)
        rows = eliminate(work[start:end, :], start)
        work[start:end, :] = rows
        if end < size:
            step = contract(rows[:, end:size], rows, 0, 0)
            work[end:, :] = work[end:, :] - step
    upper = work[:, :wide]
    upper = jnp.where(
        lax.broadcasted_iota(jnp.int32, (size, wide), 1)
        >= lax.broadcasted_iota(jnp.int32, (size, wide), 0),
        upper, 0.0,
    )
    inverse = work[:, wide:2 * wide]
    half_solved = work[:, 2 * wide:]
    margin = jnp.zeros((wide - size, wide), jnp.float32)
    inner = contract(
        jnp.concatenate([half_solved, margin], axis=0),
        jnp.concatenate([inverse, margin], axis=0), 1, 1,
    )
    whitened = 0.5 * (inner + inner.T)
    mapped = whitened[:kept]
    for iteration in range(ITERS):
        if iteration:
            mapped = contract(mapped, whitened, 1, 0)
        gram = contract(mapped, mapped, 1, 1)
        gram = jnp.concatenate([gram, jnp.zeros((kept, 128 - kept), jnp.float32)], axis=1)
        mapped = eliminate(jnp.concatenate([gram, mapped], axis=1), 0)[:, 128:]
    subspace = mapped[:, :size]
    forward = contract(subspace, inverse, 1, 0)
    backward = contract(subspace, upper, 1, 0)
    filter_ref[...] = contract(forward, backward, 0, 0)[:size, :size]


def mnf_filter(packed, size, signal_count, noise_count, kept):
    wide = packed.shape[0]
    return pl.pallas_call(
        functools.partial(mnf_kernel, 1.0 / signal_count, 1.0 / noise_count, kept),
        out_shape=jax.ShapeDtypeStruct((size, size), jnp.float32),
        in_specs=[pl.BlockSpec(memory_space=pltpu.VMEM)],
        out_specs=pl.BlockSpec(memory_space=pltpu.VMEM),
        scratch_shapes=[pltpu.VMEM((size, 3 * wide), jnp.float32)],
        name="mnf_filter",
    )(packed)


def track_place(track):
    return (lax.axis_index("line"), track)


def stats_kernel(tracks, x_ref, out_ref, paired, mine, slots, gathered, other, send, recv):
    chips = tracks // 2
    half = x_ref.shape[1] // 2
    width = x_ref.shape[2] // chips
    track = lax.axis_index("track")
    core, chip = lax.rem(track, 2), lax.div(track, 2)
    partner = track_place(chip * 2 + 1 - core)
    own_rows = pl.ds(pl.multiple_of(core * half, 8), half)
    other_rows = pl.ds(pl.multiple_of((1 - core) * half, 8), half)

    def ahead(step):
        q = lax.rem(chip + step, chips)
        return q, track_place(q * 2 + core), pl.ds(pl.multiple_of(q * width, 128), width)

    def copy(source, target, phase, sent, landed, device):
        return pltpu.make_async_remote_copy(
            src_ref=source, dst_ref=target, send_sem=send.at[phase, sent],
            recv_sem=recv.at[phase, landed], device_id=device,
            device_id_type=pl.DeviceIdType.MESH,
        )

    barrier = pltpu.get_barrier_semaphore()
    pl.semaphore_signal(barrier, inc=1, device_id=partner, device_id_type=pl.DeviceIdType.MESH)
    for step in range(1, chips):
        pl.semaphore_signal(
            barrier, inc=1, device_id=ahead(step)[1], device_id_type=pl.DeviceIdType.MESH
        )
    pl.semaphore_wait(barrier, chips)

    started = []
    for step in range(1, chips + 1):
        q, _, lanes = ahead(step)
        pair = copy(x_ref.at[:, other_rows, lanes], paired.at[q], 0, q, q, partner)
        pair.start()
        started.append(pair)
    for step in range(1, chips + 1):
        q, peer, lanes = ahead(step)
        started[step - 1].wait_recv()
        mine[q] = x_ref[:, own_rows, lanes] + paired[q]
        if step < chips:
            scatter = copy(mine.at[q], slots.at[chip], 1, q, chip, peer)
            scatter.start()
            started.append(scatter)
    total = mine[chip]
    for step in range(1, chips):
        q, peer, _ = ahead(chips - step)
        copy(mine.at[q], slots.at[q], 1, q, q, peer).wait_recv()
        total = total + slots[q]
    gathered[chip] = total
    for step in range(1, chips):
        q, peer, _ = ahead(step)
        gather = copy(gathered.at[chip], gathered.at[chip], 2, q, chip, peer)
        gather.start()
        started.append(gather)
    forward = copy(gathered.at[chip], other.at[chip], 3, chip, chip, partner)
    forward.start()
    started.append(forward)
    for step in range(1, chips):
        q, peer, _ = ahead(chips - step)
        copy(gathered.at[q], gathered.at[q], 2, q, q, peer).wait_recv()
        forward = copy(gathered.at[q], other.at[q], 3, q, q, partner)
        forward.start()
        started.append(forward)
    for q in range(chips):
        out_ref[:, own_rows, q * width:(q + 1) * width] = gathered[q]
    for q in range(chips):
        copy(other.at[q], other.at[q], 3, q, q, partner).wait_recv()
        out_ref[:, other_rows, q * width:(q + 1) * width] = other[q]
    for item in started:
        item.wait_send()


def stats_total(sums, tracks):
    chips = tracks // 2
    _, bands, lanes = sums.shape
    piece = (chips, 2, bands // 2, lanes // chips)
    return pl.pallas_call(
        functools.partial(stats_kernel, tracks),
        out_shape=jax.ShapeDtypeStruct(sums.shape, jnp.float32),
        in_specs=[pl.BlockSpec(memory_space=pltpu.VMEM)],
        out_specs=pl.BlockSpec(memory_space=pltpu.VMEM),
        scratch_shapes=[pltpu.VMEM(piece, jnp.float32)] * 5
        + [pltpu.SemaphoreType.DMA((4, chips))] * 2,
        compiler_params=pltpu.CompilerParams(collective_id=1, has_side_effects=True),
        name="stats_total",
    )(sums)


def gram_kernel(lines, tracks, x_ref, out_ref, slots, full, send, recv):
    count = lines * tracks
    me = lax.axis_index("line") * tracks + lax.axis_index("track")

    def ahead(step):
        peer = lax.rem(me + step, count)
        return peer, (lax.div(peer, tracks), lax.rem(peer, tracks))

    def settle(ref, sem):
        everyone = ref.at[pl.ds(0, count - 1)]
        pltpu.make_async_copy(everyone, everyone, sem).wait()

    barrier = pltpu.get_barrier_semaphore()

    @pl.loop(1, count)
    def _(step):
        pl.semaphore_signal(
            barrier, inc=1, device_id=ahead(step)[1], device_id_type=pl.DeviceIdType.MESH
        )

    pl.semaphore_wait(barrier, count - 1)

    @pl.loop(1, count)
    def _(step):
        peer, place = ahead(step)
        pltpu.make_async_remote_copy(
            src_ref=x_ref.at[peer], dst_ref=slots.at[me], send_sem=send.at[0],
            recv_sem=recv.at[0], device_id=place, device_id_type=pl.DeviceIdType.MESH,
        ).start()

    slots[me] = x_ref[me]
    settle(slots, recv.at[0])
    full[me] = jnp.sum(slots[...], axis=0)

    @pl.loop(1, count)
    def _(step):
        pltpu.make_async_remote_copy(
            src_ref=full.at[me], dst_ref=full.at[me], send_sem=send.at[1],
            recv_sem=recv.at[1], device_id=ahead(step)[1],
            device_id_type=pl.DeviceIdType.MESH,
        ).start()

    settle(full, recv.at[1])
    out_ref[...] = full[...]
    settle(x_ref, send.at[0])
    settle(full, send.at[1])


def gram_total(packed, lines, tracks):
    count = lines * tracks
    height, wide = packed.shape
    rows = -(-height // (8 * count)) * 8
    padded = jnp.pad(packed, ((0, count * rows - height), (0, 0)))
    piece = (count, rows, wide)
    total = pl.pallas_call(
        functools.partial(gram_kernel, lines, tracks),
        out_shape=jax.ShapeDtypeStruct(piece, jnp.float32),
        in_specs=[pl.BlockSpec(memory_space=pltpu.VMEM)],
        out_specs=pl.BlockSpec(memory_space=pltpu.VMEM),
        scratch_shapes=[pltpu.VMEM(piece, jnp.float32)] * 2
        + [pltpu.SemaphoreType.DMA((2,))] * 2,
        compiler_params=pltpu.CompilerParams(collective_id=0, has_side_effects=True),
        name="gram_total",
    )(padded.reshape(piece))
    return total.reshape(count * rows, wide)[:height]


def pack_grams(signal_part, noise_part, wide):
    size = signal_part.shape[0]
    above = jnp.arange(size)[:, None] < jnp.arange(size)[None, :]
    square = jnp.where(above, signal_part, noise_part)
    diagonal = jnp.sum(jnp.where(jnp.eye(size, dtype=bool), signal_part, 0.0), axis=0)
    packed = jnp.concatenate([square, diagonal[None]], axis=0)
    return jnp.pad(packed, ((0, wide - size - 1), (0, wide - size)))


def body(radiance):
    local_block = radiance[0]
    row_count = local_block.shape[0]
    column_count = local_block.shape[2]
    track_count = lax.axis_size("track")
    line_count = lax.axis_size("line")
    total_rows = row_count * track_count
    ahead = from_behind(local_block[:1], "track", -1)
    values = local_block.astype(jnp.float32)
    sums = jnp.stack([jnp.sum(values, axis=0), jnp.sum(values * values, axis=0)])
    strip = 128 * (track_count // 2)
    margin = -column_count % strip
    totals = stats_total(jnp.pad(sums, ((0, 0), (0, 0), (0, margin))), track_count)
    first_total, second_total = totals[0, :, :column_count], totals[1, :, :column_count]
    col_mean, factor, band_mean = column_terms(first_total, second_total, total_rows)
    centred = ((values - col_mean) * factor).astype(jnp.bfloat16)
    following = ((ahead.astype(jnp.float32) - col_mean) * factor).astype(jnp.bfloat16)
    rows_ahead = jnp.concatenate([centred[1:], following], axis=0)
    keep_last = lax.axis_index("track") < track_count - 1
    row_index = jnp.arange(row_count)
    row_keep = jnp.where((row_index < row_count - 1) | keep_last, 1.0, 0.0).astype(jnp.float32)
    differences = (
        (rows_ahead.astype(jnp.float32) - centred.astype(jnp.float32)) * row_keep[:, None, None]
    ).astype(jnp.bfloat16)
    signal_part = jnp.einsum("rbc,rdc->bd", centred, centred, preferred_element_type=jnp.float32)
    noise_part = jnp.einsum(
        "rbc,rdc->bd", differences, differences, preferred_element_type=jnp.float32
    )
    size = signal_part.shape[0]
    wide = (size // 128 + 1) * 128
    packed = gram_total(pack_grams(signal_part, noise_part, wide), line_count, track_count)
    signal_count = line_count * total_rows * column_count
    noise_count = 2 * line_count * (total_rows - 1) * column_count
    filter_matrix = mnf_filter(packed, size, signal_count, noise_count, NCOMP)
    narrow = filter_matrix.astype(jnp.bfloat16)
    mixed = jnp.einsum("ab,rac->rbc", narrow, centred, preferred_element_type=jnp.float32)
    cleaned = (band_mean[:, None] + mixed).astype(jnp.bfloat16)
    return (cleaned[None], filter_matrix)


def solution(mesh):
    in_specs = (P("line", "track", None, None),)
    out_specs = (P("line", "track", None, None), P())
    return jax.shard_map(body, mesh=mesh, in_specs=in_specs, out_specs=out_specs, check_vma=False)
```
